32 devices in a mesh: clip: 2 (over x), tm: 4 (over z), chan: 4 (over y, core).
Axes of the slice: x: 2, y: 2, z: 4, core: 2. Of those that a mesh axis runs over, the one named last changes fastest.
Arguments:
- signal: bfloat16 [2, 4096, 256], P('clip', 'tm', 'chan'), may hold values from -6 to 6
- conv_first: bfloat16 [3, 256, 128], P(None, 'chan'), may hold values from -0.21875 to 0.21875
- conv_second: bfloat16 [128, 256], P(None, 'chan'), may hold values from -0.5 to 0.5
- conv_down: bfloat16 [16, 256, 512], P(None, 'chan'), may hold values from -0.09375 to 0.09375
- cotangent: bfloat16 [2, 512, 512], P('clip', 'tm'), may hold values from -6 to 6
Outputs:
- grad_signal: bfloat16 [2, 4096, 256], P('clip', 'tm', 'chan')
- grad_first: float32 [3, 256, 128], P(None, 'chan')
- grad_second: float32 [128, 256], P(None, 'chan')
- grad_down: float32 [16, 256, 512], P(None, 'chan')
The draws below stay inside these ranges and needn't reach their ends.
All inputs are finite; a program needn't handle non-finite values.
Results may differ from the reference program's by a relative error of at most 0.018.
Values may be sent and summed in bfloat16 or wider, within the bound.
No kernel may reach another device: no remote copies, remote signals or barrier semaphores. Data moves between devices by JAX's collectives and lax.ppermute only.
A program may use at most 64 MiB of HBM per device.

```python
import jax
import jax.numpy as jnp
from jax import lax

CH = 256
HID = 128
OUTCH = 512
KRES = 3
STRIDE = 8
KDOWN = 16
CLIPS = 2
FRAMES = 4096
OUTFR = 512
RIM = 10


def steps_of(own_key, shape, shards, low, largest):
    def one(axis_at, shards_of):
        draws = jax.random.uniform(jax.random.fold_in(jax.random.fold_in(own_key, 6), axis_at), (shards_of,), jnp.float32, low / len(shards), largest / len(shards))
        return jnp.repeat(jnp.exp(draws), shape[axis_at] // shards_of).reshape((-1,) + (1,) * (len(shape) - axis_at - 1))

    loudness = one(*shards[0])
    for cut in shards[1:]:
        loudness = loudness * one(*cut)
    return loudness


def scatter_about(stream_key, shape, width, limit, pieces=(), dtype=jnp.bfloat16):
    entries = jax.random.normal(stream_key, shape, jnp.float32) * width
    if len(pieces) > 0:
        entries = steps_of(stream_key, shape, pieces, -0.22, 0.18) * entries
    return jnp.clip(entries, min=-limit, max=limit).astype(dtype)


def setup_inputs(seed: int = 0) -> dict:
    arg_keys = jax.random.split(jax.random.key(seed), 6)
    signal = scatter_about(arg_keys[0], (CLIPS, FRAMES, CH), 1.0, 6.0, ((0, 2), (1, 4), (2, 4)))
    conv_first = scatter_about(arg_keys[1], (KRES, CH, HID), (KRES * CH) ** -0.5, 0.21875, ((1, 4),))
    conv_second = scatter_about(arg_keys[2], (HID, CH), HID ** -0.5, 0.5, ((1, 4),))
    conv_down = scatter_about(arg_keys[3], (KDOWN, CH, OUTCH), (KDOWN * CH) ** -0.5, 0.09375, ((1, 4),))
    cotangent = scatter_about(arg_keys[4], (CLIPS, OUTFR, OUTCH), 1.0, 6.0, ((0, 2), (1, 4)))
    return dict(signal=signal, conv_first=conv_first, conv_second=conv_second, conv_down=conv_down, cotangent=cotangent)


def elu(value):
    return jnp.where(value > 0, value, jnp.exp(jnp.minimum(value, 0.0)) - 1.0)

def slope(value):
    return jnp.where(value > 0, 1.0, jnp.exp(jnp.minimum(value, 0.0)))

def contract_rows(left, right):
    return lax.dot_general(left, right, (((0,), (0,)), ((), ())), preferred_element_type=jnp.float32)

def contract_cols(left, right):
    return lax.dot_general(left, right, (((1,), (1,)), ((), ())), preferred_element_type=jnp.float32)

def one_clip(signal, cotangent, conv_first, conv_second, conv_down):
    frames = signal.shape[0]
    span = frames + RIM - KRES + 1
    padded = jnp.concatenate([jnp.zeros((RIM, signal.shape[1]), jnp.bfloat16), signal], axis=0)
    act = elu(padded.astype(jnp.float32)).astype(jnp.bfloat16)
    hidden = jnp.zeros((span, conv_first.shape[2]), jnp.float32)
    for k in range(KRES):
        hidden = hidden + jnp.dot(act[k:k + span], conv_first[k], preferred_element_type=jnp.float32)
    inner = elu(hidden).astype(jnp.bfloat16)
    resid = padded[KRES - 1:].astype(jnp.float32) + jnp.dot(inner, conv_second, preferred_element_type=jnp.float32)
    feed = elu(resid).astype(jnp.bfloat16)
    blocks = feed.reshape(span // STRIDE, STRIDE * signal.shape[1])
    wide = conv_down.reshape(2, STRIDE * signal.shape[1], conv_down.shape[2])
    count = cotangent.shape[0]
    front = contract_cols(cotangent, wide[0])
    back = contract_cols(cotangent, wide[1])
    dblocks = jnp.pad(front, ((0, 1), (0, 0))) + jnp.pad(back, ((1, 0), (0, 0)))
    down_raw = jnp.stack([contract_rows(blocks[:count], cotangent), contract_rows(blocks[1:], cotangent)])
    down_raw = down_raw.reshape(conv_down.shape)
    dresid = dblocks.reshape(span, signal.shape[1]) * slope(resid)
    dres16 = dresid.astype(jnp.bfloat16)
    second_raw = contract_rows(inner, dres16)
    dinner = contract_cols(dres16, conv_second)
    dhid = (dinner * slope(hidden)).astype(jnp.bfloat16)
    first_raw = jnp.stack([contract_rows(act[k:k + span], dhid) for k in range(KRES)])
    dact = jnp.zeros(padded.shape, jnp.float32)
    for k in range(KRES):
        dact = dact + jnp.pad(contract_cols(dhid, conv_first[k]), ((k, KRES - 1 - k), (0, 0)))
    dpadded = dact * slope(padded.astype(jnp.float32)) + jnp.pad(dresid, ((KRES - 1, 0), (0, 0)))
    return (dpadded[RIM:].astype(jnp.bfloat16), first_raw, second_raw, down_raw)

def reference(signal, conv_first, conv_second, conv_down, cotangent):

    def per_clip(pair):
        return one_clip(pair[0], pair[1], conv_first, conv_second, conv_down)
    grad_signal, first_raw, second_raw, down_raw = lax.map(per_clip, (signal, cotangent))
    factor = 1.0 / jnp.sqrt(jnp.float32(CLIPS * OUTFR))
    return (grad_signal, lax.optimization_barrier(jnp.sum(first_raw, axis=0)) * factor, lax.optimization_barrier(jnp.sum(second_raw, axis=0)) * factor, lax.optimization_barrier(jnp.sum(down_raw, axis=0)) * factor)
```

```python
import jax
import jax.numpy as jnp
import numpy as np
from jax import lax
from jax.experimental import pallas as pl
from jax.experimental.pallas import tpu as pltpu
from jax.sharding import PartitionSpec as P

KRES = 3
STRIDE = 8
LANE = 128
F32 = jnp.float32
BF16 = jnp.bfloat16


def dot(left, right, dims=((1,), (0,))):
    return lax.dot_general(left, right, (dims, ((), ())), preferred_element_type=F32)


def elu(value):
    return jnp.where(value > 0, value, jnp.exp(jnp.minimum(value, 0.0)) - 1.0)


def slope(value):
    return jnp.where(value > 0, 1.0, jnp.exp(jnp.minimum(value, 0.0)))


def lane_of(shape):
    return lax.broadcasted_iota(jnp.int32, shape, 1)


def roll(value, shift):
    return pltpu.roll(value, shift % value.shape[1], 1)


def swap_chunks(blocks):
    chunk = lane_of(blocks[0].shape) // 16
    blocks = list(blocks)
    for s in (1, 2, 4):
        low = (chunk & s) == 0
        new = list(blocks)
        for i in range(8):
            if i & s == 0:
                a, b = blocks[i], blocks[i | s]
                new[i] = jnp.where(low, a, roll(b, 16 * s))
                new[i | s] = jnp.where(low, roll(a, -16 * s), b)
        blocks = new
    return blocks


def interleaver():
    row = lax.broadcasted_iota(jnp.int32, (LANE, LANE), 0)
    col = lax.broadcasted_iota(jnp.int32, (LANE, LANE), 1)
    return jnp.where(col == 16 * (row % 8) + row // 8, 1.0, 0.0).astype(BF16)


def to_phase(blocks):
    rows = blocks[0].shape[0]
    mixed = dot(jnp.concatenate(blocks, axis=0), interleaver())
    return swap_chunks([mixed[rows * b : rows * (b + 1)] for b in range(8)])


def to_time(blocks):
    rows = blocks[0].shape[0]
    mixed = jnp.concatenate(swap_chunks(blocks), axis=0).astype(BF16)
    out = dot(mixed, interleaver(), ((1,), (1,)))
    return [out[rows * b : rows * (b + 1)] for b in range(8)]


def cut(value, n=8):
    return [value[:, LANE * k : LANE * (k + 1)] for k in range(n)]


def prep_kernel(sig, first, second, cot, pack, ahead, back, quarter):
    ch, length = sig.shape
    chan = lax.axis_index("chan")
    blocks = cut(sig[...])
    for k, block in enumerate(to_phase(blocks)):
        pack[:, LANE * k : LANE * (k + 1)] = block.astype(BF16)
    for k in range(KRES):
        pack[:, length + LANE * k : length + LANE * (k + 1)] = first[k]
    pack[:, length + LANE * KRES :] = second[...]
    ahead[...] = roll(blocks[7].astype(F32), 2).astype(BF16)
    back[:ch, :] = roll(blocks[0].astype(F32), 2).astype(BF16)
    head = cot[:16, :].astype(F32)
    rows = [head[r : r + 1, LANE * i : LANE * (i + 1)] for r in range(2) for i in range(4)]
    back[ch:, :] = jnp.concatenate(rows + [jnp.zeros((8, LANE), F32)], axis=0).astype(BF16)
    per = quarter.shape[0]
    quarter[...] = cot[pl.ds(pl.multiple_of(chan * per, per), per), :]


def dfeed_kernel(down, cot, ahead, back, dfeed, halo):
    ch = down.shape[1]
    width = cot.shape[1]
    tail = back[ch:, :].astype(F32)
    rows = [
        jnp.concatenate([tail[4 * r + i : 4 * r + i + 1] for i in range(4)], axis=1)
        for r in range(2)
    ]
    rows = jnp.concatenate(rows + [jnp.zeros((14, width), F32)], axis=0).astype(BF16)
    ext = jnp.concatenate(
        [cot[...], rows, jnp.zeros((LANE - 16, width), BF16)], axis=0
    )
    lane = lane_of((ch, LANE))
    ends = []
    for k in range(8):
        front = dot(down[k], ext, ((1,), (1,)))
        behind = dot(down[k + 8], ext, ((1,), (1,)))
        f0, f1 = front[:, :LANE], front[:, LANE:]
        b0, b1 = behind[:, :LANE], behind[:, LANE:]
        main = jnp.where(lane == LANE - 1, roll(f1, -1), roll(f0, -1)) + b0
        dfeed[:, LANE * k : LANE * (k + 1)] = main.astype(BF16)
        if k == 0:
            ends.append(roll(f1, -1) + b1)
        if k == 1:
            ends.append(f1 + roll(b1, 1))
    end = jnp.where(lane == 0, ends[0], jnp.where(lane == 1, ends[1], 0.0))
    dfeed[:, LANE * 8 :] = end.astype(BF16)
    near = jnp.where(lane < 2, ahead[...].astype(F32), jnp.where(lane < 4, back[:ch, :].astype(F32), 0.0))
    halo[...] = near.astype(BF16)


def forward_kernel(a0, a1, a2, a3, h0, h1, h2, h3, feed, hidden):
    packs = (a0, a1, a2, a3)
    halos = (h0, h1, h2, h3)
    ch, length = feed.shape
    taps = KRES * LANE
    act = jnp.concatenate(
        [
            jnp.concatenate([elu(a[:, :length].astype(F32)), elu(h[...].astype(F32))], axis=1)
            for a, h in zip(packs, halos)
        ],
        axis=0,
    ).astype(BF16)
    weights = jnp.concatenate([a[:, length : length + taps] for a in packs], axis=0)
    part = dot(weights, act, ((0,), (0,)))
    p0, p1, p2 = [cut(part[LANE * k : LANE * (k + 1)], 9) for k in range(KRES)]
    lane = lane_of((LANE, LANE))
    wrap6, wrap7, twice7 = roll(p0[6], 1), roll(p1[7], 1), roll(p0[7], 1)
    out = [None] * 9
    out[0] = (
        jnp.where(lane == 0, p0[8], wrap6) + jnp.where(lane == 0, roll(p1[8], -1), wrap7) + p2[0]
    )
    out[1] = jnp.where(lane == 0, roll(p0[8], -1), twice7) + p1[0] + p2[1]
    for k in range(2, 8):
        out[k] = p0[k - 2] + p1[k - 1] + p2[k]
    late = roll(p2[8], -2)
    out[8] = jnp.where(
        lane == 0,
        wrap6 + wrap7 + late,
        jnp.where(lane == 1, roll(twice7, 1) + roll(p1[8], -1) + late, 0.0),
    )
    for k in range(9):
        hidden[:, LANE * k : LANE * (k + 1)] = out[k]
    inner = elu(jnp.concatenate(out[:8], axis=1)).astype(BF16)
    resid = a0[:, :length].astype(F32) + dot(a0[:, length + taps :], inner)
    feed[...] = elu(resid).astype(BF16)


def backward_kernel(
    a0, a1, a2, a3, h0, h1, h2, h3, hidden, d0, d1, d2, d3, grad, weight
):
    packs = (a0, a1, a2, a3)
    halos = (h0, h1, h2, h3)
    grads = (d0, d1, d2, d3)
    ch, length = grad.shape
    taps = KRES * LANE
    hid = hidden[...]
    decay = jnp.exp(jnp.minimum(hid, 0.0))
    inner = jnp.where(hid > 0, hid, decay - 1.0).astype(BF16)
    hid_slope = jnp.where(hid > 0, 1.0, decay)
    mix = jnp.concatenate([a[:, length + taps :] for a in packs], axis=0)
    bent = dot(mix, inner)
    own = None
    rounded = []
    for i in range(4):
        lead = jnp.concatenate(
            [packs[i][:, :length].astype(F32), roll(halos[i][...].astype(F32), -2)], axis=1
        )
        resid = lead + bent[ch * i : ch * (i + 1)]
        dres = grads[i][...].astype(F32) * slope(resid)
        if i == 0:
            own = dres
        rounded.append(dres.astype(BF16))
    dres16 = jnp.concatenate(rounded, axis=0)
    dinner = dot(mix, dres16, ((0,), (0,)))
    dhid = (dinner * hid_slope).astype(BF16)
    weight[ch * KRES :, :] = dot(rounded[0][:, :length], inner[:, :length], ((1,), (1,))).astype(
        weight.dtype
    )
    raw = a0[:, :length].astype(F32)
    raw_decay = jnp.exp(jnp.minimum(raw, 0.0))
    act = cut(jnp.where(raw > 0, raw, raw_decay - 1.0))
    edge = elu(h0[...].astype(F32))
    lane = lane_of((ch, LANE))
    before1 = jnp.where(lane == 0, roll(edge, -1), roll(act[7], 1))
    before2 = jnp.where(lane == 0, edge, roll(act[6], 1))
    act = [v.astype(BF16) for v in [before2, before1] + act]
    stack = jnp.concatenate(
        [jnp.concatenate(act[k : k + 8], axis=1) for k in range(KRES)], axis=0
    )
    weight[: ch * KRES, :] = dot(stack, dhid[:, :length], ((1,), (1,))).astype(weight.dtype)
    taps_own = jnp.concatenate(
        [a0[:, length + LANE * k : length + LANE * (k + 1)] for k in range(KRES)], axis=0
    )
    spread = dot(taps_own, dhid)
    q0, q1, q2 = [cut(spread[ch * k : ch * (k + 1)], 9) for k in range(KRES)]
    last = lane == LANE - 1
    q1next = jnp.where(last, roll(q1[8], -1), roll(q1[0], -1))
    q0next = jnp.where(last, roll(q0[8], -1), roll(q0[0], -1))
    q0late = jnp.where(last, roll(q0[8], -2), roll(q0[1], -1))
    q0 = q0[:8] + [q0next, q0late]
    q1 = q1[:8] + [q1next]
    raw_slope = cut(jnp.where(raw > 0, 1.0, raw_decay))
    out = []
    for k in range(8):
        dact = q0[k + 2] + q1[k + 1] + q2[k]
        total = dact * raw_slope[k] + own[:, LANE * k : LANE * (k + 1)]
        out.append(total.astype(BF16).astype(F32))
    for b, block in enumerate(to_time(out)):
        grad[:, LANE * b : LANE * (b + 1)] = block.astype(BF16)


def segment(rel):
    me = lax.axis_index("clip") * lax.axis_size("tm") + lax.axis_index("tm")
    return me ^ rel


def cot_kernel(order, per_clip, q0, q1, q2, q3, out, rows):
    per = q0.shape[0] // len(order)
    width = q0.shape[1]
    chan = lax.axis_index("chan")
    for c, piece in enumerate((q0, q1, q2, q3)):
        for p, rel in enumerate(order):
            start = pl.multiple_of(segment(rel) * LANE + (chan ^ c) * per, per)
            rows[pl.ds(start, per), :] = piece[per * p : per * (p + 1), :].astype(F32)
    value = rows[...]
    out[:, :width] = value.astype(BF16)
    count = value.shape[0]
    at = lax.broadcasted_iota(jnp.int32, value.shape, 0)
    moved = jnp.where(at % per_clip == per_clip - 1, 0.0, pltpu.roll(value, count - 1, 0))
    out[:, width:] = moved.astype(BF16)


def down_kernel(order, factor, near, far, cots, out, left):
    ch = out.shape[2]
    half = len(order) // 2
    width = out.shape[3]
    for p, rel in enumerate(order):
        source = near if p < half else far
        q = p % half
        start = pl.multiple_of(segment(rel) * LANE, LANE)
        for k in range(4):
            left[ch * k : ch * (k + 1), pl.ds(start, LANE)] = source[
                ch * q : ch * (q + 1), LANE * k : LANE * (k + 1)
            ]
    total = dot(left[...], cots[...]) * factor
    for k in range(4):
        out[0, k] = total[ch * k : ch * (k + 1), width:]
        out[1, k] = total[ch * k : ch * (k + 1), :width]


def call(kernel, name, out_shape, *args, scratch=()):
    return pl.pallas_call(kernel, out_shape=out_shape, scratch_shapes=scratch, name=name)(*args)


def struct(shape, dtype=BF16):
    return jax.ShapeDtypeStruct(shape, dtype)


def down_half(index, order, factor, ch, near, far, cots, prior):
    kernel = lambda *refs: down_kernel(order, factor, *refs)
    width = cots.shape[1] // 2
    rows = cots.shape[0]
    whole = lambda v: pl.BlockSpec(v.shape, lambda i: (0,) * v.ndim)
    args = [near, far, cots]
    specs = [whole(v) for v in args]
    alias = {}
    body = kernel
    if prior is not None:
        args.append(prior)
        specs.append(pl.BlockSpec(memory_space=pl.ANY))
        alias = {3: 0}
        body = lambda n, f, c, p, o, s: kernel(n, f, c, o, s)
    return pl.pallas_call(
        body,
        grid=(1,),
        in_specs=specs,
        out_specs=pl.BlockSpec((2, 4, ch, width), lambda i: (0, index, 0, 0)),
        out_shape=struct((2, 8, ch, width), F32),
        scratch_shapes=[pltpu.VMEM((4 * ch, rows), BF16)],
        input_output_aliases=alias,
        name="down%d" % index,
    )(*args)


def along_chan(value, other):
    pairs = [(i, i ^ other) for i in range(lax.axis_size("chan"))]
    return lax.ppermute(value, "chan", pairs)


def along_group(value, other):
    count = lax.axis_size("clip") * lax.axis_size("tm")
    return lax.ppermute(value, ("clip", "tm"), [(i, i ^ other) for i in range(count)])


def shifted(value, distance):
    devices = range(lax.axis_size("tm"))
    route = [(i, i + distance) for i in devices if i + distance in devices]
    return lax.ppermute(value, "tm", route)


def after(value, *others):
    return lax.optimization_barrier((value, *others))[0]


def on_device(signal, conv_first, conv_second, conv_down, cotangent):
    sig = signal[0].T
    second = conv_second.T
    cot = cotangent[0]
    ch, length = sig.shape
    count, width = cot.shape
    clips, times = lax.axis_size("clip"), lax.axis_size("tm")
    group = clips * times
    packed = length + LANE * (KRES + 1)
    pack, ahead, back, quarter = call(
        prep_kernel,
        "prep",
        (
            struct((ch, packed)),
            struct((ch, LANE)),
            struct((ch + 16, LANE)),
            struct((count // 4, width)),
        ),
        sig,
        conv_first,
        second,
        cot,
    )
    pack_y = along_chan(pack, 2)
    ahead = shifted(ahead, 1)
    back = shifted(back, -1)
    dfeed, halo = call(
        dfeed_kernel,
        "dfeed",
        (struct((ch, length + LANE)), struct((ch, LANE))),
        conv_down,
        cot,
        ahead,
        back,
    )
    halo_y = along_chan(halo, 2)
    packs = (pack, along_chan(pack, 1), pack_y, along_chan(pack_y, 1))
    halos = (halo, along_chan(halo, 1), halo_y, along_chan(halo_y, 1))
    feed, hidden = call(
        forward_kernel,
        "forward",
        (struct((ch, length)), struct((LANE, length + LANE), F32)),
        *packs,
        *halos,
    )
    dfeed_y = along_chan(dfeed, 2)
    dfeeds = (dfeed, along_chan(dfeed, 1), dfeed_y, along_chan(dfeed_y, 1))
    grad, weight = call(
        backward_kernel,
        "backward",
        (struct((ch, length)), struct((ch * (KRES + 1), LANE))),
        *packs,
        *halos,
        hidden,
        *dfeeds,
    )
    factor = float(1.0 / np.sqrt(np.float32(clips * times * (length // STRIDE))))
    if (clips, times) == (2, 4):
        cots = jnp.concatenate([quarter, along_group(quarter, 4)])
        cots = jnp.concatenate([cots, along_group(cots, 2)])
        cots = jnp.concatenate([cots, along_group(cots, 1)])
        cots_y = along_chan(cots, 2)
        cots = pl.pallas_call(
            lambda *refs: cot_kernel((0, 4, 2, 6, 1, 5, 3, 7), times * count, *refs),
            out_shape=struct((group * count, 2 * width)),
            scratch_shapes=[pltpu.VMEM((group * count, width), F32)],
            name="cots",
        )(cots, along_chan(cots, 1), cots_y, along_chan(cots_y, 1))
        one, two = feed[:, : length // 2], feed[:, length // 2 :]
        one = jnp.concatenate([one, along_group(one, 4)])
        two = jnp.concatenate([two, along_group(two, 2)])
        one = jnp.concatenate([one, along_group(one, 2)])
        two = jnp.concatenate([two, along_group(two, 1)])
        one_far = along_group(one, 1)
        two_far = along_group(two, 4)
        down = down_half(0, (0, 4, 2, 6, 1, 5, 3, 7), factor, ch, one, one_far, cots, None)
        down = down_half(1, (0, 2, 1, 3, 4, 6, 5, 7), factor, ch, two, two_far, cots, down)
        for step in (4, 2, 1):
            other = along_group(weight, step)
            weight = weight.astype(F32) + other.astype(F32)
            if step > 1:
                weight = weight.astype(BF16)
    else:
        blocks = feed.reshape(ch, STRIDE, count).transpose(1, 0, 2).reshape(STRIDE * ch, count)
        rest = back[ch : ch + width // LANE].reshape(1, width)
        behind = dot(blocks, cot)
        front = dot(blocks, jnp.concatenate([cot[1:], rest]))
        down = jnp.stack([front, behind]) * factor
        down, weight = lax.psum((down, weight.astype(F32)), ("clip", "tm"))
    weight = weight * factor
    return (
        grad.T[None],
        weight[: ch * KRES].reshape(conv_first.shape),
        weight[ch * KRES :].T,
        down.reshape(conv_down.shape),
    )


def solution(mesh):
    return jax.shard_map(
        on_device,
        mesh=mesh,
        in_specs=(
            P("clip", "tm", "chan"),
            P(None, "chan", None),
            P(None, "chan"),
            P(None, "chan", None),
            P("clip", "tm", None),
        ),
        out_specs=(
            P("clip", "tm", "chan"),
            P(None, "chan", None),
            P(None, "chan"),
            P(None, "chan", None),
        ),
        check_vma=False,
    )
```

```python
import jax
import jax.numpy as jnp
import numpy as np
from jax import lax
from jax.experimental import pallas as pl
from jax.experimental.pallas import tpu as pltpu
from jax.sharding import PartitionSpec as P

KRES = 3
STRIDE = 8
LANE = 128
F32 = jnp.float32
BF16 = jnp.bfloat16


def dot(left, right, dims=((1,), (0,))):
    return lax.dot_general(left, right, (dims, ((), ())), preferred_element_type=F32)


def elu(value):
    return jnp.where(value > 0, value, jnp.exp(jnp.minimum(value, 0.0)) - 1.0)


def slope(value):
    return jnp.where(value > 0, 1.0, jnp.exp(jnp.minimum(value, 0.0)))


def lane_of(shape):
    return lax.broadcasted_iota(jnp.int32, shape, 1)


def roll(value, shift):
    return pltpu.roll(value, shift % value.shape[1], 1)


def swap_chunks(blocks):
    chunk = lane_of(blocks[0].shape) // 16
    blocks = list(blocks)
    for s in (1, 2, 4):
        low = (chunk & s) == 0
        new = list(blocks)
        for i in range(8):
            if i & s == 0:
                a, b = blocks[i], blocks[i | s]
                new[i] = jnp.where(low, a, roll(b, 16 * s))
                new[i | s] = jnp.where(low, roll(a, -16 * s), b)
        blocks = new
    return blocks


def interleaver():
    row = lax.broadcasted_iota(jnp.int32, (LANE, LANE), 0)
    col = lax.broadcasted_iota(jnp.int32, (LANE, LANE), 1)
    return jnp.where(col == 16 * (row % 8) + row // 8, 1.0, 0.0).astype(BF16)


def to_phase(blocks):
    rows = blocks[0].shape[0]
    mixed = dot(jnp.concatenate(blocks, axis=0), interleaver())
    return swap_chunks([mixed[rows * b : rows * (b + 1)] for b in range(8)])


def to_time(blocks):
    rows = blocks[0].shape[0]
    mixed = jnp.concatenate(swap_chunks(blocks), axis=0).astype(BF16)
    out = dot(mixed, interleaver(), ((1,), (1,)))
    return [out[rows * b : rows * (b + 1)] for b in range(8)]


def cut(value, n=8):
    return [value[:, LANE * k : LANE * (k + 1)] for k in range(n)]


def pack_kernel(sig, first, second, cot, down, pack, edge):
    ch, length = sig.shape
    blocks = cut(sig[...])
    for k, block in enumerate(to_phase(blocks)):
        pack[:, LANE * k : LANE * (k + 1)] = block.astype(BF16)
    for k in range(KRES):
        pack[:, length + LANE * k : length + LANE * (k + 1)] = first[k]
    start = length + LANE * (KRES + 1)
    pack[:, start - LANE : start] = second[...]
    lane = lane_of((ch, LANE))
    share = roll(blocks[0].astype(F32), 2)
    upstream = cot[...]
    for k in range(8):
        front = dot(down[k], upstream, ((1,), (1,)))
        back = dot(down[k + 8], upstream, ((1,), (1,)))
        share = jnp.where(lane == 4 + k, roll(front, 4 + k), share)
        if k < 2:
            share = jnp.where(lane == 12 + k, roll(front, 11 + k) + roll(back, 12 + k), share)
        main = jnp.where(lane == LANE - 1, 0.0, roll(front, -1)) + back
        pack[:, start + LANE * k : start + LANE * (k + 1)] = main.astype(BF16)
    edge[:ch, :] = roll(blocks[7].astype(F32), 2).astype(BF16)
    edge[ch:, :] = share.astype(BF16)


def merge_kernel(even, odd, halo):
    ch = halo.shape[0]
    low = lax.axis_index("tm") % 2 == 0
    lane = lane_of((ch, LANE))
    even, odd = even[...].astype(F32), odd[...].astype(F32)
    ahead = jnp.where(low, odd[:ch], even[:ch])
    back = jnp.where(low, even[ch:], odd[ch:])
    near = jnp.where(lane < 2, ahead, jnp.where(lane < 14, back, 0.0))
    halo[...] = near.astype(BF16)


def join_kernel(pack, halo, pack_y, halo_y, pair):
    ch, width = pack.shape
    pair[:ch, :width] = pack[...]
    pair[:ch, width:] = halo[...]
    pair[ch:, :width] = pack_y[...]
    pair[ch:, width:] = halo_y[...]


def forward_kernel(pair, other, one, two, hidden):
    length = 2 * one.shape[1]
    ch = one.shape[0]
    taps = length + KRES * LANE
    halo = taps + LANE + length
    pieces = [jnp.concatenate([p[:, :length], p[:, halo:]], axis=1) for p in (pair, other)]
    act = elu(jnp.concatenate(pieces, axis=0).astype(F32)).astype(BF16)
    weights = jnp.concatenate([p[:, length:taps] for p in (pair, other)], axis=0)
    part = dot(weights, act, ((0,), (0,)))
    p0, p1, p2 = [cut(part[LANE * k : LANE * (k + 1)], 9) for k in range(KRES)]
    lane = lane_of((LANE, LANE))
    wrap6, wrap7, twice7 = roll(p0[6], 1), roll(p1[7], 1), roll(p0[7], 1)
    out = [None] * 9
    out[0] = (
        jnp.where(lane == 0, p0[8], wrap6) + jnp.where(lane == 0, roll(p1[8], -1), wrap7) + p2[0]
    )
    out[1] = jnp.where(lane == 0, roll(p0[8], -1), twice7) + p1[0] + p2[1]
    for k in range(2, 8):
        out[k] = p0[k - 2] + p1[k - 1] + p2[k]
    late = roll(p2[8], -2)
    out[8] = jnp.where(
        lane == 0,
        wrap6 + wrap7 + late,
        jnp.where(lane == 1, roll(twice7, 1) + roll(p1[8], -1) + late, 0.0),
    )
    for k in range(9):
        hidden[:, LANE * k : LANE * (k + 1)] = out[k]
    inner = elu(jnp.concatenate(out[:8], axis=1)).astype(BF16)
    resid = pair[:ch, :length].astype(F32) + dot(pair[:ch, taps : taps + LANE], inner)
    feed = elu(resid).astype(BF16)
    one[...] = feed[:, : length // 2]
    two[...] = feed[:, length // 2 :]


def backward_kernel(pair, other, hidden, grad, weight):
    ch, length = grad.shape
    taps = length + KRES * LANE
    start = taps + LANE
    halo = start + length
    last = lane_of((2 * ch, LANE)) == LANE - 1
    behind = lane_of((2 * ch, LANE)) < 2
    hid = hidden[...]
    decay = jnp.exp(jnp.minimum(hid, 0.0))
    inner = jnp.where(hid > 0, hid, decay - 1.0).astype(BF16)
    hid_slope = jnp.where(hid > 0, 1.0, decay)
    mix = jnp.concatenate([p[:, taps:start] for p in (pair, other)], axis=0)
    bent = dot(mix, inner)
    own = None
    rounded = []
    for i, p in enumerate((pair, other)):
        near = p[:, halo:].astype(F32)
        lead = jnp.concatenate([p[:, :length].astype(F32), roll(near, -2)], axis=1)
        resid = lead + bent[2 * ch * i : 2 * ch * (i + 1)]
        dfeed = cut(p[:, start:halo].astype(F32))
        dfeed = [d + jnp.where(last, roll(near, LANE - 5 - k), 0.0) for k, d in enumerate(dfeed)]
        dfeed.append(jnp.where(behind, roll(near, -12), 0.0))
        dres = jnp.concatenate(dfeed, axis=1) * slope(resid)
        if i == 0:
            own = dres[:ch]
        rounded.append(dres.astype(BF16))
    dres16 = jnp.concatenate(rounded, axis=0)
    dinner = dot(mix, dres16, ((0,), (0,)))
    dhid = (dinner * hid_slope).astype(BF16)
    second = dot(rounded[0][:ch, :length], inner[:, :length], ((1,), (1,)))
    weight[:, LANE * KRES :] = second.astype(BF16)
    raw = pair[:ch, :length].astype(F32)
    raw_decay = jnp.exp(jnp.minimum(raw, 0.0))
    act = cut(jnp.where(raw > 0, raw, raw_decay - 1.0))
    edge = elu(pair[:ch, halo:].astype(F32))
    lane = lane_of((ch, LANE))
    before1 = jnp.where(lane == 0, roll(edge, -1), roll(act[7], 1))
    before2 = jnp.where(lane == 0, edge, roll(act[6], 1))
    act = [v.astype(BF16) for v in [before2, before1] + act]
    stack = jnp.concatenate(
        [jnp.concatenate(act[k : k + 8], axis=1) for k in range(KRES)], axis=0
    )
    first = dot(stack, dhid[:, :length], ((1,), (1,)))
    for k in range(KRES):
        weight[:, LANE * k : LANE * (k + 1)] = first[ch * k : ch * (k + 1)].astype(BF16)
    taps_own = jnp.concatenate(
        [pair[:ch, length + LANE * k : length + LANE * (k + 1)] for k in range(KRES)], axis=0
    )
    spread = dot(taps_own, dhid)
    q0, q1, q2 = [cut(spread[ch * k : ch * (k + 1)], 9) for k in range(KRES)]
    last = lane == LANE - 1
    q1next = jnp.where(last, roll(q1[8], -1), roll(q1[0], -1))
    q0next = jnp.where(last, roll(q0[8], -1), roll(q0[0], -1))
    q0late = jnp.where(last, roll(q0[8], -2), roll(q0[1], -1))
    q0 = q0[:8] + [q0next, q0late]
    q1 = q1[:8] + [q1next]
    raw_slope = cut(jnp.where(raw > 0, 1.0, raw_decay))
    out = []
    for k in range(8):
        dact = q0[k + 2] + q1[k + 1] + q2[k]
        total = dact * raw_slope[k] + own[:, LANE * k : LANE * (k + 1)]
        out.append(total.astype(BF16).astype(F32))
    for b, block in enumerate(to_time(out)):
        grad[:, LANE * b : LANE * (b + 1)] = block.astype(BF16)


def segment(rel):
    me = lax.axis_index("clip") * lax.axis_size("tm") + lax.axis_index("tm")
    return me ^ rel


FETCH = ((4, 3, 1, 2), (7, None, 5, 6))


def cot_kernel(per_clip, own, *refs):
    pieces, (out, rows) = refs[:2], refs[2:]
    count, width = rows.shape
    chan = lax.axis_index("chan")

    def put(rel, piece):
        start = pl.multiple_of(segment(rel) * LANE, LANE)
        rows[pl.ds(start, LANE), :] = piece[...].astype(F32)

    put(0, own)
    for c in range(4):
        for n in range(2):
            for place in range(4):
                rel = FETCH[n][place]
                if rel is not None:
                    pl.when((chan ^ c) == place)(lambda: put(rel, pieces[c % 2].at[c // 2 * 2 + n]))
    value = rows[...]
    out[:, :width] = value.astype(BF16)
    at = lax.broadcasted_iota(jnp.int32, value.shape, 0)
    moved = jnp.where(at % per_clip == per_clip - 1, 0.0, pltpu.roll(value, count - 1, 0))
    out[:, width:] = moved.astype(BF16)


def gathered(order, pieces, left):
    ch = left.shape[0] // 4
    for p in range(len(order)):
        for k in range(4):
            left[ch * k : ch * (k + 1), LANE * p : LANE * (p + 1)] = pieces[
                ch * p : ch * (p + 1), LANE * k : LANE * (k + 1)
            ]
    return left[...]


def arranged(order, cots, right):
    for p, rel in enumerate(order):
        start = pl.multiple_of(segment(rel) * LANE, LANE)
        right[LANE * p : LANE * (p + 1), :] = cots[pl.ds(start, LANE), :]
    return right[...]


def part_kernel(order, pieces, cots, out, left, right):
    out[...] = dot(gathered(order, pieces, left), arranged(order, cots, right))


def down_kernel(
    orders, factor, one, two, cots, one_part, two_part, mine, out, first, second, left, right
):
    ch = out.shape[2]
    width = out.shape[3]
    step = pl.program_id(0)
    for i, (far, part) in enumerate(((one, one_part), (two, two_part))):

        @pl.when(step == i)
        def _():
            total = dot(gathered(orders[i], far, left), arranged(orders[i], cots, right))
            total = (total + part[...]) * factor
            for k in range(4):
                out[0, k] = total[ch * k : ch * (k + 1), width:]
                out[1, k] = total[ch * k : ch * (k + 1), :width]

    @pl.when(step == 0)
    def _():
        weight = (mine[...].astype(F32) + one[4 * ch :, :].astype(F32)) * factor
        for k in range(KRES):
            first[k] = weight[:, LANE * k : LANE * (k + 1)]
        second[...] = weight[:, LANE * KRES :]


VMEM = pl.BlockSpec(memory_space=pltpu.VMEM)
LIMIT = pltpu.CompilerParams(vmem_limit_bytes=20 << 20)


def near(value):
    return pltpu.with_memory_space_constraint(value, pltpu.VMEM)


def far(value):
    return pltpu.with_memory_space_constraint(value, pltpu.HBM)


def cost(micros):
    return pl.CostEstimate(flops=0, transcendentals=0, bytes_accessed=int(micros * 3.6e6))


def whole(value):
    return pl.BlockSpec(value.shape, lambda i: (0,) * value.ndim)


def call(kernel, name, micros, out_shape, *args, loads=0, scratch=(), alias=None):
    specs = [whole(v) if i < loads else VMEM for i, v in enumerate(args)]
    args = [far(v) if i < loads else near(v) for i, v in enumerate(args)]
    return pl.pallas_call(
        kernel,
        grid=(1,),
        in_specs=specs,
        out_specs=jax.tree.map(lambda _: VMEM, out_shape),
        out_shape=jax.tree.map(lambda s: pltpu.VMEM(s.shape, s.dtype), out_shape),
        scratch_shapes=scratch,
        input_output_aliases=alias or {},
        compiler_params=LIMIT,
        cost_estimate=cost(micros),
        name=name,
    )(*args)


def struct(shape, dtype=BF16):
    return jax.ShapeDtypeStruct(shape, dtype)


def down_call(orders, factor, *args):
    ch = args[-1].shape[0]
    rows, width = args[2].shape
    width //= 2
    kernel = lambda *refs: down_kernel(orders, factor, *refs)
    return pl.pallas_call(
        kernel,
        grid=(2,),
        in_specs=[VMEM] * len(args),
        out_specs=(
            pl.BlockSpec((2, 4, ch, width), lambda i: (0, i, 0, 0)),
            pl.BlockSpec((KRES, ch, LANE), lambda i: (0, 0, 0)),
            pl.BlockSpec((ch, LANE), lambda i: (0, 0)),
        ),
        out_shape=(
            struct((2, 8, ch, width), F32),
            struct((KRES, ch, LANE), F32),
            struct((ch, LANE), F32),
        ),
        scratch_shapes=[
            pltpu.VMEM((4 * ch, rows // 2), BF16),
            pltpu.VMEM((rows // 2, 2 * width), BF16),
        ],
        compiler_params=LIMIT,
        cost_estimate=cost(2),
        name="down",
    )(*[near(v) for v in args])


def along_chan(value, other):
    pairs = [(i, i ^ other) for i in range(lax.axis_size("chan"))]
    return lax.ppermute(value, "chan", pairs)


def along_group(value, other):
    count = lax.axis_size("clip") * lax.axis_size("tm")
    return lax.ppermute(value, ("clip", "tm"), [(i, i ^ other) for i in range(count)])


def swapped(value, first):
    low = range(first, lax.axis_size("tm") - 1, 2)
    pairs = [p for i in low for p in ((i, i + 1), (i + 1, i))]
    return lax.ppermute(value, "tm", pairs)


def fetch(value, n):
    places = lax.axis_size("chan")
    pairs = []
    for me in range(lax.axis_size("clip") * lax.axis_size("tm")):
        for place in range(places):
            rel = FETCH[n][place]
            if rel is not None:
                pairs.append(((me ^ rel) * places + place, me * places + place))
    return lax.ppermute(value, ("clip", "tm", "chan"), pairs)


def after(value, *others):
    return lax.optimization_barrier((value, *others))[0]


def on_device(signal, conv_first, conv_second, conv_down, cotangent):
    sig = signal[0].T
    second = conv_second.T
    cot = cotangent[0]
    ch, length = sig.shape
    count, width = cot.shape
    clips, times = lax.axis_size("clip"), lax.axis_size("tm")
    group = clips * times
    pack, edge = call(
        pack_kernel,
        "pack",
        3,
        (
            struct((ch, 2 * length + LANE * (KRES + 1))),
            struct((2 * ch, LANE)),
        ),
        sig,
        conv_first,
        second,
        cot,
        conv_down,
        loads=5,
    )
    pack_y = along_chan(pack, 2)
    even = swapped(edge, 0)
    odd = swapped(edge, 1)
    halo = call(merge_kernel, "merge", 0.1, struct((ch, LANE)), even, odd)
    halo_y = along_chan(halo, 2)
    small = (clips, times) == (2, 4)
    fetched = ()
    if small:
        source = after(cot, edge)
        fetched = fetch(source, 0), fetch(source, 1)
    pack_y = after(pack_y, halo_y, *fetched)
    pair = call(
        join_kernel,
        "join",
        0.1,
        struct((2 * ch, 2 * length + LANE * (KRES + 2))),
        pack,
        halo,
        pack_y,
        halo_y,
    )
    other = along_chan(pair, 1)
    one, two, hidden = call(
        forward_kernel,
        "forward",
        1,
        (
            struct((ch, length // 2)),
            struct((ch, length // 2)),
            struct((LANE, length + LANE), F32),
        ),
        pair,
        other,
    )
    grad, weight = call(
        backward_kernel,
        "backward",
        2,
        (struct((ch, length)), struct((ch, LANE * (KRES + 1)))),
        pair,
        other,
        hidden,
    )
    factor = float(1.0 / np.sqrt(np.float32(clips * times * (length // STRIDE))))
    if small:
        mine = after(jnp.stack(fetched), one)
        mine = jnp.concatenate([mine, along_chan(mine, 2)])
        cots = call(
            lambda *refs: cot_kernel(times * count, *refs),
            "cots",
            1,
            struct((group * count, 2 * width)),
            cot,
            mine,
            along_chan(mine, 1),
            scratch=[pltpu.VMEM((group * count, width), F32)],
        )
        two = jnp.concatenate([two, along_group(two, 2)])
        for step in (4, 2):
            both = along_group(jnp.concatenate([one, weight]), step)
            one = jnp.concatenate([one, both[: one.shape[0]]])
            weight = weight.astype(F32) + both[-ch:].astype(F32)
            weight = weight.astype(BF16)
        two = jnp.concatenate([two, along_group(two, 1)])
        one_far = along_group(jnp.concatenate([one, weight]), 1)
        two_far = along_group(two, 4)
        parts = [
            call(
                lambda *refs: part_kernel(order, *refs),
                name,
                1,
                struct((4 * ch, 2 * width), F32),
                half,
                cots,
                scratch=[
                    pltpu.VMEM((4 * ch, 4 * count), BF16),
                    pltpu.VMEM((4 * count, 2 * width), BF16),
                ],
            )
            for order, half, name in (((0, 4, 2, 6), one, "part1"), ((0, 2, 1, 3), two, "part2"))
        ]
        down, first, second = down_call(
            ((1, 5, 3, 7), (4, 6, 5, 7)), factor, one_far, two_far, cots, *parts, weight
        )
    else:
        feed = jnp.concatenate([one, two], axis=1)
        blocks = feed.reshape(ch, STRIDE, count).transpose(1, 0, 2).reshape(STRIDE * ch, count)
        rest = lax.ppermute(cot[:1], "tm", [(i + 1, i) for i in range(times - 1)])
        behind = dot(blocks, cot)
        front = dot(blocks, jnp.concatenate([cot[1:], rest]))
        down = jnp.stack([front, behind]) * factor
        down, weight = lax.psum((down, weight.astype(F32)), ("clip", "tm"))
        weight = weight * factor
        first = jnp.stack([weight[:, LANE * k : LANE * (k + 1)] for k in range(KRES)])
        second = weight[:, LANE * KRES :]
    return (
        grad.T[None],
        first,
        second.T,
        down.reshape(conv_down.shape),
    )


def solution(mesh):
    return jax.shard_map(
        on_device,
        mesh=mesh,
        in_specs=(
            P("clip", "tm", "chan"),
            P(None, "chan", None),
            P(None, "chan"),
            P(None, "chan", None),
            P("clip", "tm", None),
        ),
        out_specs=(
            P("clip", "tm", "chan"),
            P(None, "chan", None),
            P(None, "chan"),
            P(None, "chan", None),
        ),
        check_vma=False,
    )
```

```python
import jax
import jax.numpy as jnp
import numpy as np
from jax import lax
from jax.experimental import pallas as pl
from jax.experimental.pallas import tpu as pltpu
from jax.sharding import PartitionSpec as P

KRES = 3
STRIDE = 8
LANE = 128
F32 = jnp.float32
BF16 = jnp.bfloat16


def dot(left, right, dims=((1,), (0,))):
    return lax.dot_general(left, right, (dims, ((), ())), preferred_element_type=F32)


def elu(value):
    return jnp.where(value > 0, value, jnp.exp(jnp.minimum(value, 0.0)) - 1.0)


def slope(value):
    return jnp.where(value > 0, 1.0, jnp.exp(jnp.minimum(value, 0.0)))


def lane_of(shape):
    return lax.broadcasted_iota(jnp.int32, shape, 1)


def roll(value, shift):
    return pltpu.roll(value, shift % value.shape[1], 1)


def swap_chunks(blocks):
    chunk = lane_of(blocks[0].shape) // 16
    blocks = list(blocks)
    for s in (1, 2, 4):
        low = (chunk & s) == 0
        new = list(blocks)
        for i in range(8):
            if i & s == 0:
                a, b = blocks[i], blocks[i | s]
                new[i] = jnp.where(low, a, roll(b, 16 * s))
                new[i | s] = jnp.where(low, roll(a, -16 * s), b)
        blocks = new
    return blocks


def interleaver():
    row = lax.broadcasted_iota(jnp.int32, (LANE, LANE), 0)
    col = lax.broadcasted_iota(jnp.int32, (LANE, LANE), 1)
    return jnp.where(col == 16 * (row % 8) + row // 8, 1.0, 0.0).astype(BF16)


def to_phase(blocks):
    rows = blocks[0].shape[0]
    mixed = dot(jnp.concatenate(blocks, axis=0), interleaver())
    return swap_chunks([mixed[rows * b : rows * (b + 1)] for b in range(8)])


def to_time(blocks):
    rows = blocks[0].shape[0]
    mixed = jnp.concatenate(swap_chunks(blocks), axis=0).astype(BF16)
    out = dot(mixed, interleaver(), ((1,), (1,)))
    return [out[rows * b : rows * (b + 1)] for b in range(8)]


def cut(value, n=8):
    return [value[:, LANE * k : LANE * (k + 1)] for k in range(n)]


def pack_kernel(sig, first, second, cot, down, pack, edge):
    ch, length = sig.shape
    blocks = cut(sig[...])
    for k, block in enumerate(to_phase(blocks)):
        pack[:, LANE * k : LANE * (k + 1)] = block.astype(BF16)
    for k in range(KRES):
        pack[:, length + LANE * k : length + LANE * (k + 1)] = first[k]
    start = length + LANE * (KRES + 1)
    pack[:, start - LANE : start] = second[...]
    lane = lane_of((ch, LANE))
    share = roll(blocks[0].astype(F32), 2)
    upstream = cot[...]
    for k in range(8):
        front = dot(down[k], upstream, ((1,), (1,)))
        back = dot(down[k + 8], upstream, ((1,), (1,)))
        share = jnp.where(lane == 4 + k, roll(front, 4 + k), share)
        if k < 2:
            share = jnp.where(lane == 12 + k, roll(front, 11 + k) + roll(back, 12 + k), share)
        main = jnp.where(lane == LANE - 1, 0.0, roll(front, -1)) + back
        pack[:, start + LANE * k : start + LANE * (k + 1)] = main.astype(BF16)
    edge[:ch, :] = roll(blocks[7].astype(F32), 2).astype(BF16)
    edge[ch:, :] = share.astype(BF16)


def merge_kernel(even, odd, halo):
    ch = halo.shape[0]
    low = lax.axis_index("tm") % 2 == 0
    lane = lane_of((ch, LANE))
    even, odd = even[...].astype(F32), odd[...].astype(F32)
    ahead = jnp.where(low, odd[:ch], even[:ch])
    back = jnp.where(low, even[ch:], odd[ch:])
    near = jnp.where(lane < 2, ahead, jnp.where(lane < 14, back, 0.0))
    halo[...] = near.astype(BF16)


def join_kernel(pack, halo, pack_y, halo_y, pair):
    ch, width = pack.shape
    pair[:ch, :width] = pack[...]
    pair[:ch, width:] = halo[...]
    pair[ch:, :width] = pack_y[...]
    pair[ch:, width:] = halo_y[...]


def forward_kernel(pair, other, one, two, hidden):
    length = 2 * one.shape[1]
    ch = one.shape[0]
    taps = length + KRES * LANE
    halo = taps + LANE + length
    pieces = [jnp.concatenate([p[:, :length], p[:, halo:]], axis=1) for p in (pair, other)]
    act = elu(jnp.concatenate(pieces, axis=0).astype(F32)).astype(BF16)
    weights = jnp.concatenate([p[:, length:taps] for p in (pair, other)], axis=0)
    part = dot(weights, act, ((0,), (0,)))
    p0, p1, p2 = [cut(part[LANE * k : LANE * (k + 1)], 9) for k in range(KRES)]
    lane = lane_of((LANE, LANE))
    wrap6, wrap7, twice7 = roll(p0[6], 1), roll(p1[7], 1), roll(p0[7], 1)
    out = [None] * 9
    out[0] = (
        jnp.where(lane == 0, p0[8], wrap6) + jnp.where(lane == 0, roll(p1[8], -1), wrap7) + p2[0]
    )
    out[1] = jnp.where(lane == 0, roll(p0[8], -1), twice7) + p1[0] + p2[1]
    for k in range(2, 8):
        out[k] = p0[k - 2] + p1[k - 1] + p2[k]
    late = roll(p2[8], -2)
    out[8] = jnp.where(
        lane == 0,
        wrap6 + wrap7 + late,
        jnp.where(lane == 1, roll(twice7, 1) + roll(p1[8], -1) + late, 0.0),
    )
    for k in range(9):
        hidden[:, LANE * k : LANE * (k + 1)] = out[k]
    inner = elu(jnp.concatenate(out[:8], axis=1)).astype(BF16)
    resid = pair[:ch, :length].astype(F32) + dot(pair[:ch, taps : taps + LANE], inner)
    feed = elu(resid).astype(BF16)
    one[...] = feed[:, : length // 2]
    two[...] = feed[:, length // 2 :]


def backward_kernel(pair, other, hidden, grad, weight):
    ch, length = grad.shape
    taps = length + KRES * LANE
    start = taps + LANE
    halo = start + length
    last = lane_of((2 * ch, LANE)) == LANE - 1
    behind = lane_of((2 * ch, LANE)) < 2
    hid = hidden[...]
    decay = jnp.exp(jnp.minimum(hid, 0.0))
    inner = jnp.where(hid > 0, hid, decay - 1.0).astype(BF16)
    hid_slope = jnp.where(hid > 0, 1.0, decay)
    mix = jnp.concatenate([p[:, taps:start] for p in (pair, other)], axis=0)
    bent = dot(mix, inner)
    own = None
    rounded = []
    for i, p in enumerate((pair, other)):
        near = p[:, halo:].astype(F32)
        lead = jnp.concatenate([p[:, :length].astype(F32), roll(near, -2)], axis=1)
        resid = lead + bent[2 * ch * i : 2 * ch * (i + 1)]
        dfeed = cut(p[:, start:halo].astype(F32))
        dfeed = [d + jnp.where(last, roll(near, LANE - 5 - k), 0.0) for k, d in enumerate(dfeed)]
        dfeed.append(jnp.where(behind, roll(near, -12), 0.0))
        dres = jnp.concatenate(dfeed, axis=1) * slope(resid)
        if i == 0:
            own = dres[:ch]
        rounded.append(dres.astype(BF16))
    dres16 = jnp.concatenate(rounded, axis=0)
    dinner = dot(mix, dres16, ((0,), (0,)))
    dhid = (dinner * hid_slope).astype(BF16)
    second = dot(rounded[0][:ch, :length], inner[:, :length], ((1,), (1,)))
    weight[:, LANE * KRES :] = second.astype(BF16)
    raw = pair[:ch, :length].astype(F32)
    raw_decay = jnp.exp(jnp.minimum(raw, 0.0))
    act = cut(jnp.where(raw > 0, raw, raw_decay - 1.0))
    edge = elu(pair[:ch, halo:].astype(F32))
    lane = lane_of((ch, LANE))
    before1 = jnp.where(lane == 0, roll(edge, -1), roll(act[7], 1))
    before2 = jnp.where(lane == 0, edge, roll(act[6], 1))
    act = [v.astype(BF16) for v in [before2, before1] + act]
    stack = jnp.concatenate(
        [jnp.concatenate(act[k : k + 8], axis=1) for k in range(KRES)], axis=0
    )
    first = dot(stack, dhid[:, :length], ((1,), (1,)))
    for k in range(KRES):
        weight[:, LANE * k : LANE * (k + 1)] = first[ch * k : ch * (k + 1)].astype(BF16)
    taps_own = jnp.concatenate(
        [pair[:ch, length + LANE * k : length + LANE * (k + 1)] for k in range(KRES)], axis=0
    )
    spread = dot(taps_own, dhid)
    q0, q1, q2 = [cut(spread[ch * k : ch * (k + 1)], 9) for k in range(KRES)]
    last = lane == LANE - 1
    q1next = jnp.where(last, roll(q1[8], -1), roll(q1[0], -1))
    q0next = jnp.where(last, roll(q0[8], -1), roll(q0[0], -1))
    q0late = jnp.where(last, roll(q0[8], -2), roll(q0[1], -1))
    q0 = q0[:8] + [q0next, q0late]
    q1 = q1[:8] + [q1next]
    raw_slope = cut(jnp.where(raw > 0, 1.0, raw_decay))
    out = []
    for k in range(8):
        dact = q0[k + 2] + q1[k + 1] + q2[k]
        total = dact * raw_slope[k] + own[:, LANE * k : LANE * (k + 1)]
        out.append(total.astype(BF16).astype(F32))
    for b, block in enumerate(to_time(out)):
        grad[:, LANE * b : LANE * (b + 1)] = block.astype(BF16)


def segment(rel):
    me = lax.axis_index("clip") * lax.axis_size("tm") + lax.axis_index("tm")
    return me ^ rel


FETCH = (0, 3, 1, 2)


def cot_kernel(per_clip, mine, others, out, rows):
    count, width = rows.shape
    chan = lax.axis_index("chan")
    for c in range(4):
        for clip in range(2):
            piece = (mine, others)[c % 2].at[clip * 2 + c // 2]
            for place in range(4):

                @pl.when((chan ^ c) == place)
                def _():
                    start = pl.multiple_of(segment(FETCH[place] + 4 * clip) * LANE, LANE)
                    rows[pl.ds(start, LANE), :] = piece[...].astype(F32)

    value = rows[...]
    out[:, :width] = value.astype(BF16)
    at = lax.broadcasted_iota(jnp.int32, value.shape, 0)
    moved = jnp.where(at % per_clip == per_clip - 1, 0.0, pltpu.roll(value, count - 1, 0))
    out[:, width:] = moved.astype(BF16)


def gathered(order, pieces, left):
    ch = left.shape[0] // 4
    for p in range(len(order)):
        for k in range(4):
            left[ch * k : ch * (k + 1), LANE * p : LANE * (p + 1)] = pieces[
                ch * p : ch * (p + 1), LANE * k : LANE * (k + 1)
            ]
    return left[...]


def arranged(order, cots, right):
    for p, rel in enumerate(order):
        start = pl.multiple_of(segment(rel) * LANE, LANE)
        right[LANE * p : LANE * (p + 1), :] = cots[pl.ds(start, LANE), :]
    return right[...]


def part_kernel(order, pieces, cots, out, left, right):
    out[...] = dot(gathered(order, pieces, left), arranged(order, cots, right))


def down_kernel(
    orders, factor, one, two, cots, one_part, two_part, mine, other, out, first, second, left, right
):
    ch = out.shape[2]
    width = out.shape[3]
    step = pl.program_id(0)
    for i, (far, part) in enumerate(((one, one_part), (two, two_part))):

        @pl.when(step == i)
        def _():
            total = dot(gathered(orders[i], far, left), arranged(orders[i], cots, right))
            total = (total + part[...]) * factor
            for k in range(4):
                out[0, k] = total[ch * k : ch * (k + 1), width:]
                out[1, k] = total[ch * k : ch * (k + 1), :width]

    @pl.when(step == 0)
    def _():
        weight = (mine[...].astype(F32) + other[...].astype(F32)) * factor
        for k in range(KRES):
            first[k] = weight[:, LANE * k : LANE * (k + 1)]
        second[...] = weight[:, LANE * KRES :]


VMEM = pl.BlockSpec(memory_space=pltpu.VMEM)
LIMIT = pltpu.CompilerParams(vmem_limit_bytes=20 << 20)


def near(value):
    return pltpu.with_memory_space_constraint(value, pltpu.VMEM)


def far(value):
    return pltpu.with_memory_space_constraint(value, pltpu.HBM)


def cost(micros):
    return pl.CostEstimate(flops=0, transcendentals=0, bytes_accessed=int(micros * 3.6e6))


def whole(value):
    return pl.BlockSpec(value.shape, lambda i: (0,) * value.ndim)


def call(kernel, name, micros, out_shape, *args, loads=0, scratch=(), alias=None):
    specs = [whole(v) if i < loads else VMEM for i, v in enumerate(args)]
    args = [far(v) if i < loads else near(v) for i, v in enumerate(args)]
    return pl.pallas_call(
        kernel,
        grid=(1,),
        in_specs=specs,
        out_specs=jax.tree.map(lambda _: VMEM, out_shape),
        out_shape=jax.tree.map(lambda s: pltpu.VMEM(s.shape, s.dtype), out_shape),
        scratch_shapes=scratch,
        input_output_aliases=alias or {},
        compiler_params=LIMIT,
        cost_estimate=cost(micros),
        name=name,
    )(*args)


def struct(shape, dtype=BF16):
    return jax.ShapeDtypeStruct(shape, dtype)


def down_call(orders, factor, *args):
    ch = args[-1].shape[0]
    rows, width = args[2].shape
    width //= 2
    kernel = lambda *refs: down_kernel(orders, factor, *refs)
    return pl.pallas_call(
        kernel,
        grid=(2,),
        in_specs=[VMEM] * len(args),
        out_specs=(
            pl.BlockSpec((2, 4, ch, width), lambda i: (0, i, 0, 0)),
            pl.BlockSpec((KRES, ch, LANE), lambda i: (0, 0, 0)),
            pl.BlockSpec((ch, LANE), lambda i: (0, 0)),
        ),
        out_shape=(
            struct((2, 8, ch, width), F32),
            struct((KRES, ch, LANE), F32),
            struct((ch, LANE), F32),
        ),
        scratch_shapes=[
            pltpu.VMEM((4 * ch, rows // 2), BF16),
            pltpu.VMEM((rows // 2, 2 * width), BF16),
        ],
        compiler_params=LIMIT,
        cost_estimate=cost(2),
        name="down",
    )(*[near(v) for v in args])


def along_chan(value, other):
    pairs = [(i, i ^ other) for i in range(lax.axis_size("chan"))]
    return lax.ppermute(value, "chan", pairs)


def along_group(value, other):
    count = lax.axis_size("clip") * lax.axis_size("tm")
    return lax.ppermute(value, ("clip", "tm"), [(i, i ^ other) for i in range(count)])


def swapped(value, first):
    low = range(first, lax.axis_size("tm") - 1, 2)
    pairs = [p for i in low for p in ((i, i + 1), (i + 1, i))]
    return lax.ppermute(value, "tm", pairs)


def fetch(value):
    places = lax.axis_size("chan")
    pairs = []
    for me in range(lax.axis_size("clip") * lax.axis_size("tm")):
        for place, rel in enumerate(FETCH):
            pairs.append(((me ^ rel) * places + place, me * places + place))
    return lax.ppermute(value, ("clip", "tm", "chan"), pairs)


def after(value, *others):
    return lax.optimization_barrier((value, *others))[0]


def on_device(signal, conv_first, conv_second, conv_down, cotangent):
    sig = signal[0].T
    second = conv_second.T
    cot = cotangent[0]
    ch, length = sig.shape
    count, width = cot.shape
    clips, times = lax.axis_size("clip"), lax.axis_size("tm")
    group = clips * times
    pack, edge = call(
        pack_kernel,
        "pack",
        3,
        (
            struct((ch, 2 * length + LANE * (KRES + 1))),
            struct((2 * ch, LANE)),
        ),
        sig,
        conv_first,
        second,
        cot,
        conv_down,
        loads=5,
    )
    pack_y = along_chan(pack, 2)
    even = swapped(edge, 0)
    odd = swapped(edge, 1)
    halo = call(merge_kernel, "merge", 0.1, struct((ch, LANE)), even, odd)
    halo_y = along_chan(halo, 2)
    small = (clips, times) == (2, 4)
    fetched = ()
    if small:
        source = after(cot, edge)
        fetched = (fetch(source),)
    pack_y = after(pack_y, halo_y, *fetched)
    pair = call(
        join_kernel,
        "join",
        0.1,
        struct((2 * ch, 2 * length + LANE * (KRES + 2))),
        pack,
        halo,
        pack_y,
        halo_y,
    )
    other = along_chan(pair, 1)
    one, two, hidden = call(
        forward_kernel,
        "forward",
        1,
        (
            struct((ch, length // 2)),
            struct((ch, length // 2)),
            struct((LANE, length + LANE), F32),
        ),
        pair,
        other,
    )
    grad, weight = call(
        backward_kernel,
        "backward",
        2,
        (struct((ch, length)), struct((ch, LANE * (KRES + 1)))),
        pair,
        other,
        hidden,
    )
    factor = float(1.0 / np.sqrt(np.float32(clips * times * (length // STRIDE))))
    if small:
        two = two_x = jnp.concatenate([two, along_group(two, 2)])
        both = along_group(jnp.concatenate([one, weight]), 4)
        one = one_x = jnp.concatenate([one, both[:ch]])
        weight = (weight.astype(F32) + both[ch:].astype(F32)).astype(BF16)
        one = jnp.concatenate([one, along_group(one, 2)])
        both = along_group(jnp.concatenate([two, weight]), 1)
        two = jnp.concatenate([two, both[: 2 * ch]])
        weight = (weight.astype(F32) + both[2 * ch :].astype(F32)).astype(BF16)
        mine = after(fetched[0], two_x)
        mine_y = along_chan(mine, 2)
        cross = along_group(after(fetched[0], two_x), 4)
        cross = jnp.concatenate([jnp.stack([mine, mine_y]), jnp.stack([cross, along_chan(cross, 2)])])
        cots = call(
            lambda *refs: cot_kernel(times * count, *refs),
            "cots",
            1,
            struct((group * count, 2 * width)),
            cross,
            along_chan(cross, 1),
            scratch=[pltpu.VMEM((group * count, width), F32)],
        )
        one_far = along_group(one, 1)
        two_far = along_group(two, 4)
        weights = (weight, along_group(weight, 2))
        parts = [
            call(
                lambda *refs: part_kernel(order, *refs),
                name,
                1,
                struct((4 * ch, 2 * width), F32),
                half,
                cots,
                scratch=[
                    pltpu.VMEM((4 * ch, 4 * count), BF16),
                    pltpu.VMEM((4 * count, 2 * width), BF16),
                ],
            )
            for order, half, name in (((0, 4, 2, 6), one, "part1"), ((0, 2, 1, 3), two, "part2"))
        ]
        down, first, second = down_call(
            ((1, 5, 3, 7), (4, 6, 5, 7)), factor, one_far, two_far, cots, *parts, *weights
        )
    else:
        feed = jnp.concatenate([one, two], axis=1)
        blocks = feed.reshape(ch, STRIDE, count).transpose(1, 0, 2).reshape(STRIDE * ch, count)
        rest = lax.ppermute(cot[:1], "tm", [(i + 1, i) for i in range(times - 1)])
        behind = dot(blocks, cot)
        front = dot(blocks, jnp.concatenate([cot[1:], rest]))
        down = jnp.stack([front, behind]) * factor
        down, weight = lax.psum((down, weight.astype(F32)), ("clip", "tm"))
        weight = weight * factor
        first = jnp.stack([weight[:, LANE * k : LANE * (k + 1)] for k in range(KRES)])
        second = weight[:, LANE * KRES :]
    return (
        grad.T[None],
        first,
        second.T,
        down.reshape(conv_down.shape),
    )


def solution(mesh):
    return jax.shard_map(
        on_device,
        mesh=mesh,
        in_specs=(
            P("clip", "tm", "chan"),
            P(None, "chan", None),
            P(None, "chan"),
            P(None, "chan", None),
            P("clip", "tm", None),
        ),
        out_specs=(
            P("clip", "tm", "chan"),
            P(None, "chan", None),
            P(None, "chan"),
            P(None, "chan", None),
        ),
        check_vma=False,
    )
```

```python
import jax
import jax.numpy as jnp
import numpy as np
from jax import lax
from jax.experimental import pallas as pl
from jax.experimental.pallas import tpu as pltpu
from jax.sharding import PartitionSpec as P

KRES = 3
STRIDE = 8
LANE = 128
F32 = jnp.float32
BF16 = jnp.bfloat16


def dot(left, right, dims=((1,), (0,))):
    return lax.dot_general(left, right, (dims, ((), ())), preferred_element_type=F32)


def elu(value):
    return jnp.where(value > 0, value, jnp.exp(jnp.minimum(value, 0.0)) - 1.0)


def slope(value):
    return jnp.where(value > 0, 1.0, jnp.exp(jnp.minimum(value, 0.0)))


def lane_of(shape):
    return lax.broadcasted_iota(jnp.int32, shape, 1)


def roll(value, shift):
    return pltpu.roll(value, shift % value.shape[1], 1)


def swap_chunks(blocks):
    chunk = lane_of(blocks[0].shape) // 16
    blocks = list(blocks)
    for s in (1, 2, 4):
        low = (chunk & s) == 0
        new = list(blocks)
        for i in range(8):
            if i & s == 0:
                a, b = blocks[i], blocks[i | s]
                new[i] = jnp.where(low, a, roll(b, 16 * s))
                new[i | s] = jnp.where(low, roll(a, -16 * s), b)
        blocks = new
    return blocks


def interleaver():
    row = lax.broadcasted_iota(jnp.int32, (LANE, LANE), 0)
    col = lax.broadcasted_iota(jnp.int32, (LANE, LANE), 1)
    return jnp.where(col == 16 * (row % 8) + row // 8, 1.0, 0.0).astype(BF16)


def to_phase(blocks):
    rows = blocks[0].shape[0]
    mixed = dot(jnp.concatenate(blocks, axis=0), interleaver())
    return swap_chunks([mixed[rows * b : rows * (b + 1)] for b in range(8)])


def to_time(blocks):
    rows = blocks[0].shape[0]
    mixed = jnp.concatenate(swap_chunks(blocks), axis=0).astype(BF16)
    out = dot(mixed, interleaver(), ((1,), (1,)))
    return [out[rows * b : rows * (b + 1)] for b in range(8)]


def cut(value, n=8):
    return [value[:, LANE * k : LANE * (k + 1)] for k in range(n)]


def pack_kernel(sig, first, second, cot, down, pack, edge):
    ch, length = sig.shape
    blocks = cut(sig[...])
    for k, block in enumerate(to_phase(blocks)):
        pack[:, LANE * k : LANE * (k + 1)] = block.astype(BF16)
    for k in range(KRES):
        pack[:, length + LANE * k : length + LANE * (k + 1)] = first[k]
    start = length + LANE * (KRES + 1)
    pack[:, start - LANE : start] = second[...]
    lane = lane_of((ch, LANE))
    share = roll(blocks[0].astype(F32), 2)
    upstream = cot[...]
    for k in range(8):
        front = dot(down[k], upstream, ((1,), (1,)))
        back = dot(down[k + 8], upstream, ((1,), (1,)))
        share = jnp.where(lane == 4 + k, roll(front, 4 + k), share)
        if k < 2:
            share = jnp.where(lane == 12 + k, roll(front, 11 + k) + roll(back, 12 + k), share)
        main = jnp.where(lane == LANE - 1, 0.0, roll(front, -1)) + back
        pack[:, start + LANE * k : start + LANE * (k + 1)] = main.astype(BF16)
    edge[:ch, :] = roll(blocks[7].astype(F32), 2).astype(BF16)
    edge[ch:, :] = share.astype(BF16)


def merge_kernel(even, odd, halo):
    ch = halo.shape[0]
    low = lax.axis_index("tm") % 2 == 0
    lane = lane_of((ch, LANE))
    even, odd = even[...].astype(F32), odd[...].astype(F32)
    ahead = jnp.where(low, odd[:ch], even[:ch])
    back = jnp.where(low, even[ch:], odd[ch:])
    near = jnp.where(lane < 2, ahead, jnp.where(lane < 14, back, 0.0))
    halo[...] = near.astype(BF16)


def join_kernel(pack, halo, pack_y, halo_y, pair):
    ch, width = pack.shape
    pair[:ch, :width] = pack[...]
    pair[:ch, width:] = halo[...]
    pair[ch:, :width] = pack_y[...]
    pair[ch:, width:] = halo_y[...]


def forward_kernel(pair, other, one, two, hidden):
    length = 2 * one.shape[1]
    ch = one.shape[0]
    taps = length + KRES * LANE
    halo = taps + LANE + length
    pieces = [jnp.concatenate([p[:, :length], p[:, halo:]], axis=1) for p in (pair, other)]
    act = elu(jnp.concatenate(pieces, axis=0).astype(F32)).astype(BF16)
    weights = jnp.concatenate([p[:, length:taps] for p in (pair, other)], axis=0)
    part = dot(weights, act, ((0,), (0,)))
    p0, p1, p2 = [cut(part[LANE * k : LANE * (k + 1)], 9) for k in range(KRES)]
    lane = lane_of((LANE, LANE))
    wrap6, wrap7, twice7 = roll(p0[6], 1), roll(p1[7], 1), roll(p0[7], 1)
    out = [None] * 9
    out[0] = (
        jnp.where(lane == 0, p0[8], wrap6) + jnp.where(lane == 0, roll(p1[8], -1), wrap7) + p2[0]
    )
    out[1] = jnp.where(lane == 0, roll(p0[8], -1), twice7) + p1[0] + p2[1]
    for k in range(2, 8):
        out[k] = p0[k - 2] + p1[k - 1] + p2[k]
    late = roll(p2[8], -2)
    out[8] = jnp.where(
        lane == 0,
        wrap6 + wrap7 + late,
        jnp.where(lane == 1, roll(twice7, 1) + roll(p1[8], -1) + late, 0.0),
    )
    for k in range(9):
        hidden[:, LANE * k : LANE * (k + 1)] = out[k]
    inner = elu(jnp.concatenate(out[:8], axis=1)).astype(BF16)
    resid = pair[:ch, :length].astype(F32) + dot(pair[:ch, taps : taps + LANE], inner)
    feed = elu(resid).astype(BF16)
    one[...] = feed[:, : length // 2]
    two[...] = feed[:, length // 2 :]


def backward_kernel(pair, other, hidden, grad, weight):
    ch, length = grad.shape
    taps = length + KRES * LANE
    start = taps + LANE
    halo = start + length
    last = lane_of((2 * ch, LANE)) == LANE - 1
    behind = lane_of((2 * ch, LANE)) < 2
    hid = hidden[...]
    decay = jnp.exp(jnp.minimum(hid, 0.0))
    inner = jnp.where(hid > 0, hid, decay - 1.0).astype(BF16)
    hid_slope = jnp.where(hid > 0, 1.0, decay)
    mix = jnp.concatenate([p[:, taps:start] for p in (pair, other)], axis=0)
    bent = dot(mix, inner)
    own = None
    rounded = []
    for i, p in enumerate((pair, other)):
        near = p[:, halo:].astype(F32)
        lead = jnp.concatenate([p[:, :length].astype(F32), roll(near, -2)], axis=1)
        resid = lead + bent[2 * ch * i : 2 * ch * (i + 1)]
        dfeed = cut(p[:, start:halo].astype(F32))
        dfeed = [d + jnp.where(last, roll(near, LANE - 5 - k), 0.0) for k, d in enumerate(dfeed)]
        dfeed.append(jnp.where(behind, roll(near, -12), 0.0))
        dres = jnp.concatenate(dfeed, axis=1) * slope(resid)
        if i == 0:
            own = dres[:ch]
        rounded.append(dres.astype(BF16))
    dres16 = jnp.concatenate(rounded, axis=0)
    dinner = dot(mix, dres16, ((0,), (0,)))
    dhid = (dinner * hid_slope).astype(BF16)
    second = dot(rounded[0][:ch, :length], inner[:, :length], ((1,), (1,)))
    weight[:, LANE * KRES :] = second.astype(BF16)
    raw = pair[:ch, :length].astype(F32)
    raw_decay = jnp.exp(jnp.minimum(raw, 0.0))
    act = cut(jnp.where(raw > 0, raw, raw_decay - 1.0))
    edge = elu(pair[:ch, halo:].astype(F32))
    lane = lane_of((ch, LANE))
    before1 = jnp.where(lane == 0, roll(edge, -1), roll(act[7], 1))
    before2 = jnp.where(lane == 0, edge, roll(act[6], 1))
    act = [v.astype(BF16) for v in [before2, before1] + act]
    stack = jnp.concatenate(
        [jnp.concatenate(act[k : k + 8], axis=1) for k in range(KRES)], axis=0
    )
    first = dot(stack, dhid[:, :length], ((1,), (1,)))
    for k in range(KRES):
        weight[:, LANE * k : LANE * (k + 1)] = first[ch * k : ch * (k + 1)].astype(BF16)
    taps_own = jnp.concatenate(
        [pair[:ch, length + LANE * k : length + LANE * (k + 1)] for k in range(KRES)], axis=0
    )
    spread = dot(taps_own, dhid)
    q0, q1, q2 = [cut(spread[ch * k : ch * (k + 1)], 9) for k in range(KRES)]
    last = lane == LANE - 1
    q1next = jnp.where(last, roll(q1[8], -1), roll(q1[0], -1))
    q0next = jnp.where(last, roll(q0[8], -1), roll(q0[0], -1))
    q0late = jnp.where(last, roll(q0[8], -2), roll(q0[1], -1))
    q0 = q0[:8] + [q0next, q0late]
    q1 = q1[:8] + [q1next]
    raw_slope = cut(jnp.where(raw > 0, 1.0, raw_decay))
    out = []
    for k in range(8):
        dact = q0[k + 2] + q1[k + 1] + q2[k]
        total = dact * raw_slope[k] + own[:, LANE * k : LANE * (k + 1)]
        out.append(total.astype(BF16).astype(F32))
    for b, block in enumerate(to_time(out)):
        grad[:, LANE * b : LANE * (b + 1)] = block.astype(BF16)


def segment(rel):
    me = lax.axis_index("clip") * lax.axis_size("tm") + lax.axis_index("tm")
    return me ^ rel


FETCH = (0, 3, 1, 2)


def cot_kernel(per_clip, mine, others, out, rows):
    count, width = rows.shape
    chan = lax.axis_index("chan")
    for c in range(4):
        for clip in range(2):
            piece = (mine, others)[c % 2].at[clip * 2 + c // 2]
            for place in range(4):

                @pl.when((chan ^ c) == place)
                def _():
                    start = pl.multiple_of(segment(FETCH[place] + 4 * clip) * LANE, LANE)
                    rows[pl.ds(start, LANE), :] = piece[...].astype(F32)

    value = rows[...]
    out[:, :width] = value.astype(BF16)
    at = lax.broadcasted_iota(jnp.int32, value.shape, 0)
    moved = jnp.where(at % per_clip == per_clip - 1, 0.0, pltpu.roll(value, count - 1, 0))
    out[:, width:] = moved.astype(BF16)


def gathered(order, pieces, left):
    ch = left.shape[0] // 4
    for p in range(len(order)):
        for k in range(4):
            left[ch * k : ch * (k + 1), LANE * p : LANE * (p + 1)] = pieces[
                ch * p : ch * (p + 1), LANE * k : LANE * (k + 1)
            ]
    return left[...]


def arranged(order, cots, right):
    for p, rel in enumerate(order):
        start = pl.multiple_of(segment(rel) * LANE, LANE)
        right[LANE * p : LANE * (p + 1), :] = cots[pl.ds(start, LANE), :]
    return right[...]


def part_kernel(order, later, pieces, cots, out, rows, left, right):
    out[...] = dot(gathered(order, pieces, left), arranged(order, cots, right))
    arranged(later, cots, rows)


def down_kernel(
    orders, factor, one, two, one_part, one_rows, two_part, two_rows, mine, other, out, first, second, left
):
    ch = out.shape[2]
    width = out.shape[3]
    step = pl.program_id(0)
    for i, (far, part, rows) in enumerate(((one, one_part, one_rows), (two, two_part, two_rows))):

        @pl.when(step == i)
        def _():
            total = dot(gathered(orders[i], far, left), rows[...])
            total = (total + part[...]) * factor
            for k in range(4):
                out[0, k] = total[ch * k : ch * (k + 1), width:]
                out[1, k] = total[ch * k : ch * (k + 1), :width]

    @pl.when(step == 0)
    def _():
        weight = (mine[...].astype(F32) + other[...].astype(F32)) * factor
        for k in range(KRES):
            first[k] = weight[:, LANE * k : LANE * (k + 1)]
        second[...] = weight[:, LANE * KRES :]


VMEM = pl.BlockSpec(memory_space=pltpu.VMEM)
LIMIT = pltpu.CompilerParams(vmem_limit_bytes=20 << 20)


def near(value):
    return pltpu.with_memory_space_constraint(value, pltpu.VMEM)


def far(value):
    return pltpu.with_memory_space_constraint(value, pltpu.HBM)


def cost(micros):
    return pl.CostEstimate(flops=0, transcendentals=0, bytes_accessed=int(micros * 3.6e6))


def whole(value):
    return pl.BlockSpec(value.shape, lambda i: (0,) * value.ndim)


def call(kernel, name, micros, out_shape, *args, loads=0, scratch=(), alias=None):
    specs = [whole(v) if i < loads else VMEM for i, v in enumerate(args)]
    args = [far(v) if i < loads else near(v) for i, v in enumerate(args)]
    return pl.pallas_call(
        kernel,
        grid=(1,),
        in_specs=specs,
        out_specs=jax.tree.map(lambda _: VMEM, out_shape),
        out_shape=jax.tree.map(lambda s: pltpu.VMEM(s.shape, s.dtype), out_shape),
        scratch_shapes=scratch,
        input_output_aliases=alias or {},
        compiler_params=LIMIT,
        cost_estimate=cost(micros),
        name=name,
    )(*args)


def struct(shape, dtype=BF16):
    return jax.ShapeDtypeStruct(shape, dtype)


def down_call(orders, factor, *args):
    ch = args[-1].shape[0]
    rows, width = args[3].shape
    width //= 2
    kernel = lambda *refs: down_kernel(orders, factor, *refs)
    return pl.pallas_call(
        kernel,
        grid=(2,),
        in_specs=[VMEM] * len(args),
        out_specs=(
            pl.BlockSpec((2, 4, ch, width), lambda i: (0, i, 0, 0)),
            pl.BlockSpec((KRES, ch, LANE), lambda i: (0, 0, 0)),
            pl.BlockSpec((ch, LANE), lambda i: (0, 0)),
        ),
        out_shape=(
            struct((2, 8, ch, width), F32),
            struct((KRES, ch, LANE), F32),
            struct((ch, LANE), F32),
        ),
        scratch_shapes=[
            pltpu.VMEM((4 * ch, rows), BF16),
        ],
        compiler_params=LIMIT,
        cost_estimate=cost(2),
        name="down",
    )(*[near(v) for v in args])


def along_chan(value, other):
    pairs = [(i, i ^ other) for i in range(lax.axis_size("chan"))]
    return lax.ppermute(value, "chan", pairs)


def along_group(value, other):
    count = lax.axis_size("clip") * lax.axis_size("tm")
    return lax.ppermute(value, ("clip", "tm"), [(i, i ^ other) for i in range(count)])


def swapped(value, first):
    low = range(first, lax.axis_size("tm") - 1, 2)
    pairs = [p for i in low for p in ((i, i + 1), (i + 1, i))]
    return lax.ppermute(value, "tm", pairs)


def fetch(value):
    places = lax.axis_size("chan")
    pairs = []
    for me in range(lax.axis_size("clip") * lax.axis_size("tm")):
        for place, rel in enumerate(FETCH):
            pairs.append(((me ^ rel) * places + place, me * places + place))
    return lax.ppermute(value, ("clip", "tm", "chan"), pairs)


def after(value, *others):
    return lax.optimization_barrier((value, *others))[0]


def on_device(signal, conv_first, conv_second, conv_down, cotangent):
    sig = signal[0].T
    second = conv_second.T
    cot = cotangent[0]
    ch, length = sig.shape
    count, width = cot.shape
    clips, times = lax.axis_size("clip"), lax.axis_size("tm")
    group = clips * times
    pack, edge = call(
        pack_kernel,
        "pack",
        3,
        (
            struct((ch, 2 * length + LANE * (KRES + 1))),
            struct((2 * ch, LANE)),
        ),
        sig,
        conv_first,
        second,
        cot,
        conv_down,
        loads=5,
    )
    pack_y = along_chan(pack, 2)
    even = swapped(edge, 0)
    odd = swapped(edge, 1)
    halo = call(merge_kernel, "merge", 0.1, struct((ch, LANE)), even, odd)
    halo_y = along_chan(halo, 2)
    small = (clips, times) == (2, 4)
    fetched = ()
    if small:
        source = after(cot, edge)
        fetched = (fetch(source),)
    pack_y = after(pack_y, halo_y, *fetched)
    pair = call(
        join_kernel,
        "join",
        0.1,
        struct((2 * ch, 2 * length + LANE * (KRES + 2))),
        pack,
        halo,
        pack_y,
        halo_y,
    )
    other = along_chan(pair, 1)
    one, two, hidden = call(
        forward_kernel,
        "forward",
        1,
        (
            struct((ch, length // 2)),
            struct((ch, length // 2)),
            struct((LANE, length + LANE), F32),
        ),
        pair,
        other,
    )
    grad, weight = call(
        backward_kernel,
        "backward",
        2,
        (struct((ch, length)), struct((ch, LANE * (KRES + 1)))),
        pair,
        other,
        hidden,
    )
    factor = float(1.0 / np.sqrt(np.float32(clips * times * (length // STRIDE))))
    if small:
        two = two_x = jnp.concatenate([two, along_group(two, 2)])
        both = along_group(jnp.concatenate([one, weight]), 4)
        one = one_x = jnp.concatenate([one, both[:ch]])
        weight = (weight.astype(F32) + both[ch:].astype(F32)).astype(BF16)
        one = jnp.concatenate([one, along_group(one, 2)])
        both = along_group(jnp.concatenate([two, weight]), 1)
        two = jnp.concatenate([two, both[: 2 * ch]])
        weight = (weight.astype(F32) + both[2 * ch :].astype(F32)).astype(BF16)
        mine = after(fetched[0], two_x)
        mine_y = along_chan(mine, 2)
        cross = along_group(after(fetched[0], two_x), 4)
        cross = jnp.concatenate([jnp.stack([mine, mine_y]), jnp.stack([cross, along_chan(cross, 2)])])
        cots = call(
            lambda *refs: cot_kernel(times * count, *refs),
            "cots",
            1,
            struct((group * count, 2 * width)),
            cross,
            along_chan(cross, 1),
            scratch=[pltpu.VMEM((group * count, width), F32)],
        )
        one_far = along_group(one, 1)
        two_far = along_group(two, 4)
        weights = (weight, along_group(weight, 2))
        near_orders = ((0, 4, 2, 6), (0, 2, 1, 3))
        far_orders = ((1, 5, 3, 7), (4, 6, 5, 7))
        parts = []
        for order, later, half, name in zip(near_orders, far_orders, (one, two), ("part1", "part2")):
            parts += call(
                lambda *refs: part_kernel(order, later, *refs),
                name,
                1,
                (struct((4 * ch, 2 * width), F32), struct((4 * count, 2 * width))),
                half,
                cots,
                scratch=[
                    pltpu.VMEM((4 * ch, 4 * count), BF16),
                    pltpu.VMEM((4 * count, 2 * width), BF16),
                ],
            )
        down, first, second = down_call(far_orders, factor, one_far, two_far, *parts, *weights)
    else:
        feed = jnp.concatenate([one, two], axis=1)
        blocks = feed.reshape(ch, STRIDE, count).transpose(1, 0, 2).reshape(STRIDE * ch, count)
        rest = lax.ppermute(cot[:1], "tm", [(i + 1, i) for i in range(times - 1)])
        behind = dot(blocks, cot)
        front = dot(blocks, jnp.concatenate([cot[1:], rest]))
        down = jnp.stack([front, behind]) * factor
        down, weight = lax.psum((down, weight.astype(F32)), ("clip", "tm"))
        weight = weight * factor
        first = jnp.stack([weight[:, LANE * k : LANE * (k + 1)] for k in range(KRES)])
        second = weight[:, LANE * KRES :]
    return (
        grad.T[None],
        first,
        second.T,
        down.reshape(conv_down.shape),
    )


def solution(mesh):
    return jax.shard_map(
        on_device,
        mesh=mesh,
        in_specs=(
            P("clip", "tm", "chan"),
            P(None, "chan", None),
            P(None, "chan"),
            P(None, "chan", None),
            P("clip", "tm", None),
        ),
        out_specs=(
            P("clip", "tm", "chan"),
            P(None, "chan", None),
            P(None, "chan"),
            P(None, "chan", None),
        ),
        check_vma=False,
    )
```
